128 devices in a mesh: atom: 32 (over z, y, core), dp: 4 (over x).
Axes of the slice: x: 4, y: 4, z: 4, core: 2. Of those that a mesh axis runs over, the one named last changes fastest.
Arguments:
- activations: bfloat16 [512, 8192], P('dp'), may hold values from -6 to 6
- dictionary: bfloat16 [8192, 65536], P('dp', 'atom'), may hold values from -0.03535534 to 0.03535534
Outputs:
- sparse_codes: float32 [512, 65536], P('dp', 'atom')
- residual: float32 [512, 8192], P('atom', 'dp')
- new_dictionary: bfloat16 [8192, 65536], P('dp', 'atom')
The draws below stay inside these ranges and needn't reach their ends.
All inputs are finite; a program needn't handle non-finite values.
Results may differ from the reference program's by a relative error of at most 0.0025.
Values may be sent and summed in bfloat16 or wider, within the bound.
No kernel may reach another device: no remote copies, remote signals or barrier semaphores. Data moves between devices by JAX's collectives and lax.ppermute only.
A program may use at most 128 MiB of HBM per device.

```python
import math
import jax
import jax.numpy as jnp
from jax import lax

D = 8192
ATOMS = 65536
ITERS = 2
ROWS = 512


def draw_dictionary(key, part):
    keys = jax.random.split(jax.random.fold_in(key, 11), 3)
    base = jax.random.truncated_normal(keys[0], -4.0, 4.0, (D, ATOMS), jnp.float32)
    feature_pos = jnp.arange(D, dtype=jnp.float32) / float(max(D - 1, 1))
    row_scale = 10.0 ** jax.random.uniform(keys[1], (D, 1), jnp.float32) * jnp.sqrt(1.0 + 2.0 * feature_pos)[:, None]
    col_scale = 10.0 ** jax.random.uniform(keys[2], (1, ATOMS), jnp.float32)
    return (base * row_scale * col_scale * 0.0046 / jnp.sqrt(float(D))).astype(jnp.bfloat16)


def level_of(stream_key, extent, pieces, least, top_value):
    gain, own = 1.0, jax.random.fold_in(stream_key, 6)
    for axis_at, shards_of in pieces:
        steps = jnp.exp(jax.random.uniform(jax.random.fold_in(own, axis_at), (shards_of,), jnp.float32, least / len(pieces), top_value / len(pieces)))
        gain = gain * jnp.repeat(steps, extent[axis_at] // shards_of).reshape([-1 if axis == axis_at else 1 for axis in range(len(extent))])
    return gain


def scatter_about(key, extent, scale, limit, cuts=(), held_as=jnp.bfloat16):
    loudness = level_of(key, extent, cuts, -0.22, 0.18) if cuts else 1.0
    result = jax.random.normal(key, extent, jnp.float32) * scale * loudness
    return jnp.minimum(jnp.maximum(result, -limit), limit).astype(held_as)


def setup_inputs(seed: int = 0) -> dict:
    arg_keys = jax.random.split(jax.random.key(seed), 3)
    activations = scatter_about(arg_keys[0], (ROWS, D), 1.0, 6.0, ((0, 4),))
    dictionary = draw_dictionary(jax.random.fold_in(arg_keys[2], 71), 0)
    return dict(activations=activations, dictionary=dictionary)


threshold = 0.05
step_size = 2.0
learn_rate = 1.0 / 16384.0
epsilon = 1e-12

def shrink(values):
    return values - jnp.clip(values, -threshold, threshold)

def product(left, right):
    return jnp.dot(left.astype(jnp.float32), right.astype(jnp.float32), precision=lax.Precision.HIGHEST, preferred_element_type=jnp.float32)

def residual_of(inputs, coded, dict_wide):
    recon = product(coded, dict_wide.T)
    full_residual = inputs - recon
    return (full_residual.astype(jnp.bfloat16), full_residual)

def reference(activations, dictionary):
    inputs = activations.astype(jnp.float32)
    dict_wide = dictionary.astype(jnp.float32)
    sparse_codes = jnp.zeros((ROWS, ATOMS), jnp.float32)
    rounded = activations
    coded = None
    for iteration in range(ITERS):
        if iteration > 0:
            rounded, residual = residual_of(inputs, coded, dict_wide)
        drive_term = product(rounded, dict_wide)
        sparse_codes = shrink(sparse_codes + step_size * drive_term)
        coded = sparse_codes.astype(jnp.bfloat16)
    rounded, residual = residual_of(inputs, coded, dict_wide)
    block_size = math.gcd(ATOMS, 4096)
    block_count = ATOMS // block_size
    weight_blocks = dictionary.reshape(D, block_count, block_size).transpose(1, 0, 2)
    code_blocks = coded.reshape(ROWS, block_count, block_size).transpose(1, 0, 2)
    rounded_t = rounded.T

    def update(blocks_pair):
        weight_block, code_block = blocks_pair
        gradient = product(rounded_t, code_block)
        shifted = weight_block.astype(jnp.float32) + learn_rate * gradient
        mean_square = lax.optimization_barrier(jnp.mean(shifted * shifted, axis=0))
        return (shifted * lax.rsqrt(mean_square + epsilon)).astype(jnp.bfloat16)
    updated = lax.map(update, (weight_blocks, code_blocks))
    new_dictionary = updated.transpose(1, 0, 2).reshape(D, ATOMS)
    return (sparse_codes, residual, new_dictionary)
```

```python
import jax
import jax.numpy as jnp
from jax import lax
from jax.sharding import Mesh, PartitionSpec as P

D = 8192
ITERS = 2
threshold = 0.05
step_size = 2.0
learn_rate = 1.0 / 16384.0
epsilon = 1e-12

BF = jnp.bfloat16
F32 = jnp.float32
ATOM = ("z", "y", "core")


def shrink(values):
    return values - jnp.clip(values, -threshold, threshold)


def dot(left, right, dims):
    return lax.dot_general(left, right, (dims, ((), ())), preferred_element_type=F32)


def shift_x(value, step):
    return lax.ppermute(value, "x", [(i, (i + step) % 4) for i in range(4)])


def other_core(value):
    return lax.ppermute(value, "core", [(0, 1), (1, 0)])


def mixed(step, first):
    pairs = []
    for z in range(4):
        for y in range(4):
            for core in range(2):
                along_y = (core == 0) == first
                to_z, to_y = (z, (y + step) % 4) if along_y else ((z + step) % 4, y)
                pairs.append((z * 8 + y * 2 + core, to_z * 8 + to_y * 2 + core))
    return pairs


def shift_mixed(value, step, first):
    return lax.ppermute(value, ATOM, mixed(step, first))


def at(stack, index):
    return lax.dynamic_index_in_dim(stack, index, 0, keepdims=False)


def place(own_index, pieces):
    order = [lax.rem(own_index - t + 4, 4) for t in range(4)]
    return jnp.stack([lax.select_n(order[t], *pieces) for t in range(4)])


def body(activations, dictionary):
    x = lax.axis_index("x")
    y = lax.axis_index("y")
    z = lax.axis_index("z")
    core = lax.axis_index("core")
    first_index = jnp.where(core == 0, y, z)
    second_index = jnp.where(core == 0, z, y)
    rows, atoms = activations.shape[0], dictionary.shape[1]
    feats = dictionary.shape[0]

    half = lax.dynamic_slice_in_dim(activations, core * (rows // 2), rows // 2, 0)
    own_block = lax.dynamic_slice_in_dim(activations, x * feats, feats, 1)
    halves = [
        shift_x(
            lax.dynamic_slice_in_dim(half, lax.rem(x + k, 4) * feats, feats, 1), k
        )
        for k in (1, 2, 3)
    ]
    mine = jnp.stack(halves)
    others = other_core(mine)
    low = jnp.where(core == 0, mine, others)
    high = jnp.where(core == 0, others, mine)
    blocks = [own_block] + [
        jnp.concatenate([low[k], high[k]], axis=0) for k in range(3)
    ]
    inputs = place(x, blocks)

    def residual_of(coded):
        recon = dot(coded, dictionary, ((1,), (1,)))
        recon = recon.reshape(4, 4, 2, 16, feats)
        part0 = recon[:, :, 0].transpose(1, 0, 2, 3)
        part1 = recon[:, :, 1]
        keep = jnp.where(core == 0, part0, part1)
        send = jnp.where(core == 0, part1, part0).astype(BF)
        keep = (keep + other_core(send).astype(F32)).astype(BF)
        pieces = [
            shift_mixed(at(keep, lax.rem(first_index + k, 4)), k, True)
            for k in (2, 1, 3)
        ]
        total = at(keep, first_index).astype(F32)
        for piece in pieces:
            total = total + piece.astype(F32)
        total = total.astype(BF)
        pieces = [shift_mixed(total, k, False) for k in (2, 1, 3)]
        total = total.astype(F32)
        for piece in pieces:
            total = total + piece.astype(F32)
        acts = inputs.reshape(4, 4, 2, 16, feats)
        acts0 = lax.dynamic_index_in_dim(acts[:, :, 0], y, 1, keepdims=False)
        acts1 = lax.dynamic_index_in_dim(acts[:, :, 1], z, 0, keepdims=False)
        full = jnp.where(core == 0, acts0, acts1).astype(F32) - total
        own = at(full, second_index)
        rounded = full.astype(BF)
        gathered = place(
            first_index,
            [rounded] + [shift_mixed(rounded, k, True) for k in (1, 2, 3)],
        )
        partner = other_core(gathered)
        part0 = jnp.where(core == 0, gathered, partner).transpose(1, 0, 2, 3)
        part1 = jnp.where(core == 0, partner, gathered)
        both = jnp.stack([part0, part1], axis=2)
        return both.reshape(4, rows, feats), own

    sparse_codes = None
    rounded = inputs
    for iteration in range(ITERS):
        received = [
            shift_x(dot(at(rounded, lax.rem(x + k, 4)), dictionary, ((1,), (0,))).astype(BF), k)
            for k in (2, 1, 3)
        ]
        drive = dot(at(rounded, x), dictionary, ((1,), (0,)))
        for piece in received:
            drive = drive + piece.astype(F32)
        before = step_size * drive
        sparse_codes = shrink(before if iteration == 0 else sparse_codes + before)
        coded_own = sparse_codes.astype(BF)
        up, down = shift_x(coded_own, 1), shift_x(coded_own, -1)
        far = jnp.concatenate(
            [shift_x(up[: rows // 2], 1), shift_x(down[rows // 2 :], -1)], axis=0
        )
        coded = place(x, [coded_own, up, far, down]).reshape(4 * rows, atoms)
        rounded, residual = residual_of(coded)
    gradient = dot(rounded.reshape(4 * rows, feats), coded, ((0,), (0,)))
    updated = dictionary.astype(F32) + learn_rate * gradient
    squares = lax.psum(jnp.sum(updated * updated, axis=0), "x")
    new_dictionary = (updated * lax.rsqrt(squares / D + epsilon)).astype(BF)
    return (sparse_codes, residual, new_dictionary)


def solution(mesh):
    mesh = Mesh(mesh.devices.reshape(4, 4, 2, 4), ("z", "y", "core", "x"))
    return jax.shard_map(
        body,
        mesh=mesh,
        in_specs=(P("x", None), P("x", ATOM)),
        out_specs=(P("x", ATOM), P(ATOM, "x"), P("x", ATOM)),
        check_vma=False,
    )
```

```python
import functools

import jax
import jax.numpy as jnp
from jax import lax
from jax.experimental import pallas as pl
from jax.experimental.pallas import tpu as pltpu
from jax.sharding import Mesh, PartitionSpec as P


D = 8192
ITERS = 2
threshold = 0.05
step_size = 2.0
learn_rate = 1.0 / 16384.0
epsilon = 1e-12

BF = jnp.bfloat16
F32 = jnp.float32
ATOM = ("z", "y", "core")
MIB = 1 << 20


def shrink(values):
    return values - jnp.clip(values, -threshold, threshold)


def shift_x(value, step):
    return lax.ppermute(value, "x", [(i, (i + step) % 4) for i in range(4)])


def other_core(value):
    return lax.ppermute(value, "core", [(0, 1), (1, 0)])


def pairs_of(target):
    return [
        (z * 8 + y * 2 + core, target(z, y, core))
        for z in range(4)
        for y in range(4)
        for core in range(2)
    ]


def shift_mixed(value, step, first):
    def target(z, y, core):
        if (core == 0) == first:
            y = (y + step) % 4
        else:
            z = (z + step) % 4
        return z * 8 + y * 2 + core

    return lax.ppermute(value, ATOM, pairs_of(target))


def to_owner(value):
    def target(z, y, core):
        row, part = (y, z) if core == 0 else (z, y)
        return row * 8 + (2 * core + part // 2) * 2 + part % 2

    return lax.ppermute(value, ATOM, pairs_of(target))


def whole():
    return pl.BlockSpec(memory_space=pltpu.VMEM)


def anywhere():
    return pl.BlockSpec(memory_space=pl.ANY)


def scalars():
    return pl.BlockSpec(memory_space=pltpu.SMEM)


def in_vmem(value):
    return pltpu.with_memory_space_constraint(value, pltpu.VMEM)


def params(mib):
    return pltpu.CompilerParams(vmem_limit_bytes=mib * MIB)


def cost(flops, moved):
    return pl.CostEstimate(flops=flops, bytes_accessed=moved, transcendentals=0)


def shaped(rows, columns, dtype):
    return jax.ShapeDtypeStruct((rows, columns), dtype)


STRIP = 16


def strip(i):
    return pl.ds(pl.multiple_of(i * STRIP, STRIP), STRIP)


def fetch(index, pieces, target, sem, wait):
    for t, piece in enumerate(pieces):

        @pl.when(index == t)
        def _():
            copy = pltpu.make_async_copy(piece, target, sem)
            if wait:
                copy.wait()
            else:
                copy.start()


def encode_kernel(count, k, index_ref, *refs):
    own, other = refs[:count], refs[count : 2 * count]
    dict_ref, out_ref, left, sems = refs[2 * count :]
    half = left.shape[0] // 2
    own_at = index_ref[k, 0] if count > 1 else 0
    other_at = index_ref[k, 1] if count > 1 else 0
    for wait in (False, True):
        fetch(own_at, own, left.at[pl.ds(0, half)], sems.at[0], wait)
        fetch(other_at, other, left.at[pl.ds(half, half)], sems.at[1], wait)
    out_ref[...] = jnp.dot(
        left[...], dict_ref[...], preferred_element_type=F32
    ).astype(out_ref.dtype)


def encode_block(own, other, index, k, dictionary, dtype):
    half, feats = own[0].shape
    atoms = dictionary.shape[1]
    return pl.pallas_call(
        functools.partial(encode_kernel, len(own), k),
        in_specs=[scalars()] + [anywhere()] * (2 * len(own)) + [whole()],
        out_specs=whole(),
        out_shape=shaped(2 * half, atoms, dtype),
        scratch_shapes=[
            pltpu.VMEM((2 * half, feats), BF),
            pltpu.SemaphoreType.DMA((2,)),
        ],
        compiler_params=params(12),
        cost_estimate=cost(4 * half * feats * atoms, 2 * feats * atoms),
        name="encode",
    )(index, *own, *other, in_vmem(dictionary))


def finish_kernel(last, index_ref, drive_ref, *refs):
    received, refs = refs[:3], refs[3:]
    before_ref = refs[0] if last else None
    codes_ref, coded_ref = refs[-2:]
    rows = drive_ref.shape[0]

    @pl.loop(0, rows // STRIP)
    def _(i):
        here = strip(i)
        drive = drive_ref[here, :]
        for piece in received:
            drive = drive + piece[here, :].astype(F32)
        drive = step_size * drive
        codes = shrink(before_ref[here, :] + drive if last else drive)
        there = here
        if last:
            there = strip(lax.rem(i + index_ref[4, 1] * (rows // STRIP // 2), rows // STRIP))
        codes_ref[there, :] = codes
        coded_ref[here, :] = codes.astype(BF)


def finish(index, drive, received, before):
    rows, atoms = drive.shape
    last = before is not None
    return pl.pallas_call(
        functools.partial(finish_kernel, last),
        in_specs=[scalars()] + [whole()] * (5 if last else 4),
        out_specs=[whole()] * 2,
        out_shape=[shaped(rows, atoms, F32), shaped(rows, atoms, BF)],
        compiler_params=params(12),
        cost_estimate=cost(8 * rows * atoms, 16 * rows * atoms),
        name="finish",
    )(index, drive, *received, *([before] if last else []))


def decode_kernel(count, *refs):
    coded, dict_ref, keeps = refs[:count], refs[count], refs[count + 1 : -2]
    send_ref, left = refs[-2:]
    base = 0
    for piece in coded:
        left[pl.ds(base, piece.shape[0]), :] = piece[...]
        base += piece.shape[0]
    half = keeps[0].shape[0]
    recon = lax.dot_general(
        left[...], dict_ref[...], (((1,), (1,)), ((), ())), preferred_element_type=F32
    )
    for b, keep in enumerate(keeps):
        keep[...] = recon[2 * b * half : (2 * b + 1) * half]
        send_ref[pl.ds(b * half, half), :] = recon[
            (2 * b + 1) * half : (2 * b + 2) * half
        ].astype(BF)


def decode_blocks(coded, dictionary, half):
    feats, atoms = dictionary.shape
    rows = sum(piece.shape[0] for piece in coded)
    count = rows // 2 // half
    outs = pl.pallas_call(
        functools.partial(decode_kernel, len(coded)),
        in_specs=[whole()] * (len(coded) + 1),
        out_specs=[whole()] * (count + 1),
        out_shape=[shaped(half, feats, F32)] * count + [shaped(rows // 2, feats, BF)],
        scratch_shapes=[
            pltpu.VMEM((rows, atoms), BF),
        ],
        compiler_params=params(12),
        cost_estimate=cost(2 * rows * feats * atoms, 2 * feats * atoms),
        name="decode",
    )(*coded, in_vmem(dictionary))
    return outs[:-1], outs[-1]


def route_kernel(index_ref, *refs):
    keeps, (sent_own, sent_pair, sent_far), outs = refs[:4], refs[4:7], refs[7:]
    half = outs[0].shape[0]
    sources = [(sent_own, 0), (sent_pair, 0), (sent_far, 0), (sent_pair, half)]
    for j in range(4):
        source, base = sources[j]

        @pl.loop(0, half // STRIP)
        def _(i):
            here = strip(i)
            there = pl.ds(pl.multiple_of(base + i * STRIP, STRIP), STRIP)
            value = (keeps[j][here, :] + source[there, :].astype(F32)).astype(BF)
            for k in range(4):

                @pl.when(index_ref[k, 2] == j)
                def _():
                    outs[k][here, :] = value


def route(index, keeps, sent):
    half, feats = keeps[0].shape
    return pl.pallas_call(
        route_kernel,
        in_specs=[scalars()] + [whole()] * 7,
        out_specs=[whole()] * 4,
        out_shape=[shaped(half, feats, BF)] * 4,
        compiler_params=params(12),
        cost_estimate=cost(8 * half * feats, 32 * half * feats),
        name="route",
    )(index, *keeps, *sent)


def total_of(pieces, here):
    total = pieces[0][here, :].astype(F32)
    for piece in pieces[1:]:
        total = total + piece[here, :].astype(F32)
    return total


def partial_kernel(*refs):
    @pl.loop(0, refs[0].shape[0] // STRIP)
    def _(i):
        refs[-1][strip(i), :] = total_of(refs[:-1], strip(i)).astype(BF)


def partial_sum(pieces):
    half, feats = pieces[0].shape
    return pl.pallas_call(
        partial_kernel,
        in_specs=[whole()] * 4,
        out_specs=whole(),
        out_shape=shaped(half, feats, BF),
        compiler_params=params(8),
        cost_estimate=cost(4 * half * feats, 10 * half * feats),
        name="partial",
    )(*pieces)


def residual_kernel(index_ref, *refs):
    pieces, acts = refs[:4], refs[4:8]
    rounded_ref, mine_ref, act, sem = refs[8:]
    for wait in (False, True):
        fetch(index_ref[0, 2], acts, act, sem, wait)

    @pl.loop(0, act.shape[0] // STRIP)
    def _(i):
        here = strip(i)
        full = act[here, :].astype(F32) - total_of(pieces, here)
        rounded_ref[here, :] = full.astype(BF)

        @pl.when(i == index_ref[4, 0])
        def _():
            mine_ref[...] = full


def residual_block(index, pieces, acts):
    half, feats = pieces[0].shape
    return pl.pallas_call(
        residual_kernel,
        in_specs=[scalars()] + [whole()] * 4 + [anywhere()] * 4,
        out_specs=[whole()] * 2,
        out_shape=[shaped(half, feats, BF), shaped(STRIP, feats, F32)],
        scratch_shapes=[pltpu.VMEM((half, feats), BF), pltpu.SemaphoreType.DMA],
        compiler_params=params(8),
        cost_estimate=cost(5 * half * feats, 14 * half * feats),
        name="residual",
    )(index, *pieces, *acts)


def gradient_kernel(index_ref, *refs):
    own, other, coded = refs[:4], refs[4:8], refs[8:15]
    dict_ref, moved_ref, square_ref, turned, stage, sems = refs[15:]
    half = own[0].shape[0]
    for wait in (False, True):
        for j in range(4):
            k = (4 - j) % 4
            low, high = pl.ds(0, half), pl.ds(half, half)
            fetch(index_ref[k, 0], own, stage.at[j, low], sems.at[j, 0], wait)
            fetch(index_ref[k, 1], other, stage.at[j, high], sems.at[j, 1], wait)
    for j in range(4):
        turned[:, pl.ds(j * 2 * half, 2 * half)] = stage[j].T
    feats = dict_ref.shape[0]
    size, block = 512, 512

    @pl.loop(0, dict_ref.shape[1] // size)
    def _(n):
        part = pl.ds(pl.multiple_of(n * size, size), size)
        codes = jnp.concatenate([piece[:, part] for piece in coded], axis=0)

        def step(f, total):
            rows = pl.ds(pl.multiple_of(f * block, block), block)
            grad = jnp.dot(turned[rows, :], codes, preferred_element_type=F32)
            moved = dict_ref[rows, part].astype(F32) + learn_rate * grad
            moved_ref[rows, part] = moved
            return total + jnp.sum(moved * moved, axis=0, keepdims=True)

        square_ref[:, part] = lax.fori_loop(0, feats // block, step, jnp.zeros((1, size), F32))


def gradient(own, other, index, coded, dictionary):
    feats, atoms = dictionary.shape
    half = own[0].shape[0]
    return pl.pallas_call(
        gradient_kernel,
        in_specs=[scalars()] + [anywhere()] * 8 + [whole()] * 8,
        out_specs=[whole()] * 2,
        out_shape=[pltpu.VMEM((feats, atoms), F32), shaped(1, atoms, F32)],
        scratch_shapes=[
            pltpu.VMEM((feats, 8 * half), BF),
            pltpu.VMEM((4, 2 * half, feats), BF),
            pltpu.SemaphoreType.DMA((4, 2)),
        ],
        compiler_params=params(30),
        cost_estimate=cost(16 * half * feats * atoms, 6 * feats * atoms),
        name="gradient",
    )(index, *own, *other, *coded, in_vmem(dictionary))


def scale_kernel(moved_ref, *refs):
    squares, out_ref = refs[:4], refs[-1]
    square = squares[0][...] + squares[1][...] + squares[2][...] + squares[3][...]
    size = out_ref.shape[0]
    rows = pl.ds(pl.multiple_of(pl.program_id(0) * size, size), size)
    factor = lax.rsqrt(square / D + epsilon)
    out_ref[...] = (moved_ref[rows, :] * factor).astype(BF)


def scale(moved, squares):
    feats, atoms = moved.shape
    block = 256
    return pl.pallas_call(
        scale_kernel,
        grid=(feats // block,),
        in_specs=[whole()] * 5,
        out_specs=pl.BlockSpec((block, atoms), lambda i: (i, 0)),
        out_shape=shaped(feats, atoms, BF),
        compiler_params=params(12),
        cost_estimate=cost(feats * atoms, feats * atoms * 2),
        name="scale",
    )(in_vmem(moved), *squares)


def step(activations, dictionary):
    x = lax.axis_index("x")
    y = lax.axis_index("y")
    z = lax.axis_index("z")
    core = lax.axis_index("core")
    first = jnp.where(core == 0, y, z)
    second = jnp.where(core == 0, z, y)
    rows = activations.shape[0]
    feats = dictionary.shape[0]
    half = rows // 2
    steps = jnp.arange(4, dtype=jnp.int32)[:, None]
    base = jnp.stack([first - x, second - x, x - first])[None]
    index = jnp.concatenate(
        [lax.rem(base - steps + 8, 4), jnp.stack([second, core, core])[None]], axis=0
    )

    def act_of(part, block):
        return lax.dynamic_slice(activations, (part * half, block * feats), (half, feats))

    own_act = [act_of(core, x), None, None, None]
    other_act = [act_of(1 - core, x), None, None, None]
    for k in (1, 3, 2):
        own_act[k] = shift_x(act_of(core, lax.rem(x + k, 4)), k)
    for k in (1, 3, 2):
        other_act[k] = other_core(own_act[k])

    def encode(source, order, before):
        def part(k, dtype):
            own, other = source(k)
            return encode_block(own, other, index, k, dictionary, dtype)

        received = []
        for k in order:
            sent = part(k, BF)
            received.append(shift_x(sent, k))
        drive = part(0, F32)
        return finish(index, drive, received, before)

    def gather(coded):
        low, high = coded[:half], coded[half:]
        up_low = shift_x(low, 1)
        down_high = shift_x(high, -1)
        up_high = shift_x(high, 1)
        down_low = shift_x(low, -1)
        far_low = shift_x(up_low, 1)
        far_high = shift_x(down_high, -1)
        return (coded,), (up_low, up_high), (far_low, far_high), (down_low, down_high)

    def residual_of(coded):
        keeps, sent = [None] * 4, []
        for blocks in ((0,), (1, 3), (2,)):
            pieces = [piece for j in blocks for piece in coded[j]]
            kept, send = decode_blocks(pieces, dictionary, half)
            for j, keep in zip(blocks, kept):
                keeps[j] = keep
            sent.append(other_core(send))
        routed = route(index, keeps, sent)
        pieces = [routed[0]]
        for k in (2, 1, 3):
            pieces.append(shift_mixed(routed[k], k, True))
        total = partial_sum(pieces)
        pieces = [total]
        for k in (2, 1, 3):
            pieces.append(shift_mixed(total, k, False))
        rounded, mine = residual_block(index, pieces, own_act)
        own = [rounded, None, None, None]
        other = [None] * 4
        for k in (2, 1, 3):
            own[k] = shift_mixed(rounded, k, True)
        for k in (0, 1, 3, 2):
            other[k] = other_core(own[k])
        return mine, own, other

    codes = None
    source = lambda k: (own_act[(4 - k) % 4 :][:1], other_act[(4 - k) % 4 :][:1])
    for iteration in range(ITERS):
        order = (3, 1, 2) if iteration == 0 else (2, 1, 3)
        codes, coded = encode(source, order, codes)
        coded = gather(coded)
        mine, own, other = residual_of(coded)
        source = lambda k, own=own, other=other: (own, other)

    residual = to_owner(mine)
    flat = [coded[0][0], *coded[1], *coded[2], *coded[3]]
    moved, square = gradient(own, other, index, flat, dictionary)
    squares = [square]
    for k in (2, 1, 3):
        squares.append(shift_x(square, k))
    new_dictionary = scale(moved, squares)
    return (codes, residual, new_dictionary)


def solution(mesh):
    mesh = Mesh(mesh.devices.reshape(4, 4, 2, 4), ("z", "y", "core", "x"))
    return jax.shard_map(
        step,
        mesh=mesh,
        in_specs=(P("x", None), P("x", ATOM)),
        out_specs=(P("x", ATOM), P(ATOM, "x"), P("x", ATOM)),
        check_vma=False,
    )
```

```python
import functools

import jax
import jax.numpy as jnp
from jax import lax
from jax.experimental import pallas as pl
from jax.experimental.pallas import tpu as pltpu
from jax.sharding import Mesh, PartitionSpec as P


D = 8192
ITERS = 2
threshold = 0.05
step_size = 2.0
learn_rate = 1.0 / 16384.0
epsilon = 1e-12

BF = jnp.bfloat16
F32 = jnp.float32
ATOM = ("z", "y", "core")
MIB = 1 << 20


def shrink(values):
    return values - jnp.clip(values, -threshold, threshold)


def shift_x(value, step):
    return lax.ppermute(value, "x", [(i, (i + step) % 4) for i in range(4)])


def other_core(value):
    return lax.ppermute(value, "core", [(0, 1), (1, 0)])


def pairs_of(target):
    return [
        (z * 8 + y * 2 + core, target(z, y, core))
        for z in range(4)
        for y in range(4)
        for core in range(2)
    ]


def shift_mixed(value, step, first):
    def target(z, y, core):
        if (core == 0) == first:
            y = (y + step) % 4
        else:
            z = (z + step) % 4
        return z * 8 + y * 2 + core

    return lax.ppermute(value, ATOM, pairs_of(target))


def to_owner(value):
    def target(z, y, core):
        row, part = (y, z) if core == 0 else (z, y)
        return row * 8 + (2 * core + part // 2) * 2 + part % 2

    return lax.ppermute(value, ATOM, pairs_of(target))


def whole():
    return pl.BlockSpec(memory_space=pltpu.VMEM)


def anywhere():
    return pl.BlockSpec(memory_space=pl.ANY)


def scalars():
    return pl.BlockSpec(memory_space=pltpu.SMEM)


def in_vmem(value):
    return pltpu.with_memory_space_constraint(value, pltpu.VMEM)


def params(mib):
    return pltpu.CompilerParams(vmem_limit_bytes=mib * MIB)


def cost(flops, moved):
    return pl.CostEstimate(flops=flops, bytes_accessed=moved, transcendentals=0)


def shaped(rows, columns, dtype):
    return jax.ShapeDtypeStruct((rows, columns), dtype)


STRIP = 16


def strip(i):
    return pl.ds(pl.multiple_of(i * STRIP, STRIP), STRIP)


def fetch(index, pieces, target, sem, wait):
    for t, piece in enumerate(pieces):

        @pl.when(index == t)
        def _():
            copy = pltpu.make_async_copy(piece, target, sem)
            if wait:
                copy.wait()
            else:
                copy.start()


def load_kernel(dict_ref, out_ref, sem):
    copy = pltpu.make_async_copy(dict_ref, out_ref, sem)
    copy.start()
    copy.wait()


def load(dictionary):
    return pl.pallas_call(
        load_kernel,
        in_specs=[pl.BlockSpec(memory_space=pltpu.HBM)],
        out_specs=whole(),
        out_shape=pltpu.VMEM(dictionary.shape, BF),
        scratch_shapes=[pltpu.SemaphoreType.DMA],
        compiler_params=params(10),
        cost_estimate=cost(0, dictionary.size * 2),
        name="load",
    )(pltpu.with_memory_space_constraint(dictionary, pltpu.HBM))


def encode_kernel(size, count, k, index_ref, *refs):
    own, other = refs[:count], refs[count : 2 * count]
    dict_ref, low_ref, high_ref, left, sems = refs[2 * count :]
    half = left.shape[0] // 2
    own_at = index_ref[k, 0] if count > 1 else 0
    other_at = index_ref[k, 1] if count > 1 else 0
    for wait in (False, True):
        fetch(own_at, own, left.at[pl.ds(0, half)], sems.at[0], wait)
        fetch(other_at, other, left.at[pl.ds(half, half)], sems.at[1], wait)

    @pl.loop(0, dict_ref.shape[1] // size)
    def _(n):
        part = pl.ds(pl.multiple_of(n * size, size), size)
        out = jnp.dot(left[...], dict_ref[:, part], preferred_element_type=F32)
        low_ref[:, part] = out[:half].astype(low_ref.dtype)
        high_ref[:, part] = out[half:].astype(high_ref.dtype)


def encode_block(own, other, index, k, dictionary, size):
    half, feats = own[0].shape
    atoms = dictionary.shape[1]
    low = BF if k in (2, 3) else F32
    high = BF if k in (1, 2) else F32
    return pl.pallas_call(
        functools.partial(encode_kernel, size, len(own), k),
        in_specs=[scalars()] + [anywhere()] * (2 * len(own)) + [whole()],
        out_specs=[whole()] * 2,
        out_shape=[shaped(half, atoms, low), shaped(half, atoms, high)],
        scratch_shapes=[
            pltpu.VMEM((2 * half, feats), BF),
            pltpu.SemaphoreType.DMA((2,)),
        ],
        compiler_params=params(12),
        cost_estimate=cost(4 * half * feats * atoms, 2 * feats * atoms),
        name="encode",
    )(index, *own, *other, in_vmem(dictionary))


def add_kernel(sum_ref, piece_ref, out_ref):
    @pl.loop(0, sum_ref.shape[0] // STRIP)
    def _(i):
        here = strip(i)
        out_ref[here, :] = (sum_ref[here, :] + piece_ref[here, :].astype(F32)).astype(BF)


def add(total, piece):
    half, atoms = total.shape
    return pl.pallas_call(
        add_kernel,
        in_specs=[whole()] * 2,
        out_specs=whole(),
        out_shape=shaped(half, atoms, BF),
        compiler_params=params(8),
        cost_estimate=cost(half * atoms, 8 * half * atoms),
        name="add",
    )(in_vmem(total), piece)


def finish_kernel(last, index_ref, *refs):
    drives, received, refs = refs[:2], (refs[2:4], refs[4:6]), refs[6:]
    before_ref = refs[0] if last else None
    codes_ref, *coded = refs[-3:]
    half = drives[0].shape[0]
    strips = half // STRIP
    for h in range(2):

        @pl.loop(0, strips)
        def _(i):
            here, kept = strip(i), strip(i + h * strips)
            drive = drives[h][here, :]
            for piece in received[h]:
                drive = drive + piece[here, :].astype(F32)
            drive = step_size * drive
            codes = shrink(before_ref[kept, :] + drive if last else drive)
            there = kept
            if last:
                there = strip(lax.rem(i + (h + index_ref[4, 1]) * strips, 2 * strips))
            codes_ref[there, :] = codes
            coded[h][here, :] = codes.astype(BF)


def finish(index, drives, received, before):
    half, atoms = drives[0].shape
    last = before is not None
    codes, *coded = pl.pallas_call(
        functools.partial(finish_kernel, last),
        in_specs=[scalars()] + [whole()] * (7 if last else 6),
        out_specs=[whole()] * 3,
        out_shape=[shaped(2 * half, atoms, F32)] + [shaped(half, atoms, BF)] * 2,
        compiler_params=params(12),
        cost_estimate=cost(16 * half * atoms, 32 * half * atoms),
        name="finish",
    )(index, *drives, *received, *([in_vmem(before)] if last else []))
    return codes, coded


def decode_kernel(size, count, *refs):
    coded, dict_ref, keeps = refs[:count], refs[count], refs[count + 1 : -2]
    send_ref, left = refs[-2:]
    base = 0
    for piece in coded:
        left[pl.ds(base, piece.shape[0]), :] = piece[...]
        base += piece.shape[0]
    half = keeps[0].shape[0]

    @pl.loop(0, dict_ref.shape[0] // size)
    def _(n):
        part = pl.ds(pl.multiple_of(n * size, size), size)
        recon = lax.dot_general(
            left[...], dict_ref[part, :], (((1,), (1,)), ((), ())), preferred_element_type=F32
        )
        for b, keep in enumerate(keeps):
            keep[:, part] = recon[2 * b * half : (2 * b + 1) * half]
            send_ref[pl.ds(b * half, half), part] = recon[
                (2 * b + 1) * half : (2 * b + 2) * half
            ].astype(BF)


def decode_blocks(coded, dictionary, half, size):
    feats, atoms = dictionary.shape
    rows = sum(piece.shape[0] for piece in coded)
    count = rows // 2 // half
    outs = pl.pallas_call(
        functools.partial(decode_kernel, size, len(coded)),
        in_specs=[whole()] * (len(coded) + 1),
        out_specs=[whole()] * (count + 1),
        out_shape=[shaped(half, feats, F32)] * count + [shaped(rows // 2, feats, BF)],
        scratch_shapes=[
            pltpu.VMEM((rows, atoms), BF),
        ],
        compiler_params=params(12),
        cost_estimate=cost(2 * rows * feats * atoms, 2 * feats * atoms),
        name="decode",
    )(*coded, in_vmem(dictionary))
    return outs[:-1], outs[-1]


def route_kernel(index_ref, *refs):
    keeps, (sent_own, sent_pair, sent_far), outs = refs[:4], refs[4:7], refs[7:]
    half = outs[0].shape[0]
    sources = [(sent_own, 0), (sent_pair, 0), (sent_far, 0), (sent_pair, half)]
    for j in range(4):
        source, base = sources[j]

        @pl.loop(0, half // STRIP)
        def _(i):
            here = strip(i)
            there = pl.ds(pl.multiple_of(base + i * STRIP, STRIP), STRIP)
            value = (keeps[j][here, :] + source[there, :].astype(F32)).astype(BF)
            for k in range(4):

                @pl.when(index_ref[k, 2] == j)
                def _():
                    outs[k][here, :] = value


def route(index, keeps, sent):
    half, feats = keeps[0].shape
    return pl.pallas_call(
        route_kernel,
        in_specs=[scalars()] + [whole()] * 7,
        out_specs=[whole()] * 4,
        out_shape=[shaped(half, feats, BF)] * 4,
        compiler_params=params(12),
        cost_estimate=cost(8 * half * feats, 32 * half * feats),
        name="route",
    )(index, *keeps, *sent)


def total_of(pieces, here):
    total = pieces[0][here, :].astype(F32)
    for piece in pieces[1:]:
        total = total + piece[here, :].astype(F32)
    return total


def partial_kernel(*refs):
    @pl.loop(0, refs[0].shape[0] // STRIP)
    def _(i):
        refs[-1][strip(i), :] = total_of(refs[:-1], strip(i)).astype(BF)


def partial_sum(pieces):
    half, feats = pieces[0].shape
    return pl.pallas_call(
        partial_kernel,
        in_specs=[whole()] * 4,
        out_specs=whole(),
        out_shape=shaped(half, feats, BF),
        compiler_params=params(8),
        cost_estimate=cost(4 * half * feats, 10 * half * feats),
        name="partial",
    )(*pieces)


def residual_kernel(index_ref, *refs):
    pieces, acts = refs[:4], refs[4:8]
    rounded_ref, mine_ref, act, sem = refs[8:]
    for wait in (False, True):
        fetch(index_ref[0, 2], acts, act, sem, wait)

    @pl.loop(0, act.shape[0] // STRIP)
    def _(i):
        here = strip(i)
        full = act[here, :].astype(F32) - total_of(pieces, here)
        rounded_ref[here, :] = full.astype(BF)

        @pl.when(i == index_ref[4, 0])
        def _():
            mine_ref[...] = full


def residual_block(index, pieces, acts):
    half, feats = pieces[0].shape
    return pl.pallas_call(
        residual_kernel,
        in_specs=[scalars()] + [whole()] * 4 + [anywhere()] * 4,
        out_specs=[whole()] * 2,
        out_shape=[shaped(half, feats, BF), shaped(STRIP, feats, F32)],
        scratch_shapes=[pltpu.VMEM((half, feats), BF), pltpu.SemaphoreType.DMA],
        compiler_params=params(8),
        cost_estimate=cost(5 * half * feats, 14 * half * feats),
        name="residual",
    )(index, *pieces, *acts)


def arrange_kernel(index_ref, *refs):
    low, high, out_ref, sems = refs[:4], refs[4:8], refs[8], refs[9]
    half = low[0].shape[0]
    for wait in (False, True):
        for k in range(4):
            back = (4 - k) % 4
            own, other = pl.ds(2 * k * half, half), pl.ds((2 * k + 1) * half, half)
            fetch(index_ref[back, 2], low, out_ref.at[own], sems.at[k, 0], wait)
            fetch(index_ref[back, 3], high, out_ref.at[other], sems.at[k, 1], wait)


def arrange(index, coded):
    half, atoms = coded[0][0].shape
    low, high = zip(*coded)
    return pl.pallas_call(
        arrange_kernel,
        in_specs=[scalars()] + [anywhere()] * 8,
        out_specs=whole(),
        out_shape=pltpu.VMEM((8 * half, atoms), BF),
        scratch_shapes=[pltpu.SemaphoreType.DMA((4, 2))],
        compiler_params=params(8),
        cost_estimate=cost(0, 32 * half * atoms),
        name="arrange",
    )(index, *low, *high)


def turn_kernel(own_ref, other_ref, out_ref):
    out_ref[...] = jnp.concatenate([own_ref[...], other_ref[...]], axis=0).T


def turn(own, other):
    half, feats = own.shape
    return pl.pallas_call(
        turn_kernel,
        in_specs=[whole()] * 2,
        out_specs=whole(),
        out_shape=pltpu.VMEM((feats, 2 * half), BF),
        compiler_params=params(8),
        cost_estimate=cost(0, 8 * half * feats),
        name="turn",
    )(own, other)


def gradient_kernel(*refs):
    turned, (codes_ref, dict_ref, moved_ref, square_ref) = refs[:4], refs[4:]
    feats = dict_ref.shape[0]
    size, block = 512, 512

    @pl.loop(0, dict_ref.shape[1] // size)
    def _(n):
        part = pl.ds(pl.multiple_of(n * size, size), size)
        codes = codes_ref[:, part]
        total = jnp.zeros((8, size), F32)
        for f in range(feats // block):
            rows = pl.ds(f * block, block)
            left = jnp.concatenate([piece[rows, :] for piece in turned], axis=1)
            grad = jnp.dot(left, codes, preferred_element_type=F32)
            moved = dict_ref[rows, part].astype(F32) + learn_rate * grad
            moved_ref[rows, part] = moved
            total = total + jnp.sum((moved * moved).reshape(block // 8, 8, size), axis=0)
        square_ref[:, part] = jnp.sum(total, axis=0, keepdims=True)


def gradient(turned, codes, dictionary):
    feats, atoms = dictionary.shape
    rows = codes.shape[0]
    return pl.pallas_call(
        gradient_kernel,
        in_specs=[whole()] * 6,
        out_specs=[whole()] * 2,
        out_shape=[pltpu.VMEM((feats, atoms), F32), shaped(1, atoms, F32)],
        compiler_params=params(30),
        cost_estimate=cost(2 * rows * feats * atoms, 6 * feats * atoms),
        name="gradient",
    )(*(in_vmem(piece) for piece in turned), in_vmem(codes), in_vmem(dictionary))


def scale_kernel(moved_ref, *refs):
    squares, (out_ref, ready, sems) = refs[:4], refs[4:]
    square = squares[0][...] + squares[1][...] + squares[2][...] + squares[3][...]
    factor = lax.rsqrt(square / D + epsilon)
    count, block, _ = ready.shape
    copies = []
    for n in range(count):
        rows = pl.ds(n * block, block)

        @pl.loop(0, block // STRIP)
        def _(i):
            from_rows = pl.ds(pl.multiple_of(n * block + i * STRIP, STRIP), STRIP)
            ready[n, strip(i), :] = (moved_ref[from_rows, :] * factor).astype(BF)

        copies.append(pltpu.make_async_copy(ready.at[n], out_ref.at[rows], sems.at[n]))
        copies[n].start()
    for copy in copies:
        copy.wait()


def scale(moved, squares):
    feats, atoms = moved.shape
    count = 8
    return pl.pallas_call(
        scale_kernel,
        in_specs=[whole()] * 5,
        out_specs=pl.BlockSpec(memory_space=pltpu.HBM),
        out_shape=shaped(feats, atoms, BF),
        scratch_shapes=[
            pltpu.VMEM((count, feats // count, atoms), BF),
            pltpu.SemaphoreType.DMA((count,)),
        ],
        compiler_params=params(16),
        cost_estimate=cost(feats * atoms, feats * atoms * 2),
        name="scale",
    )(in_vmem(moved), *squares)


def step(activations, dictionary):
    x = lax.axis_index("x")
    y = lax.axis_index("y")
    z = lax.axis_index("z")
    core = lax.axis_index("core")
    first = jnp.where(core == 0, y, z)
    second = jnp.where(core == 0, z, y)
    rows = activations.shape[0]
    feats = dictionary.shape[0]
    half = rows // 2
    steps = jnp.arange(4, dtype=jnp.int32)[:, None]
    base = jnp.stack([first - x, second - x, x - first, x - second])[None]
    index = jnp.concatenate(
        [lax.rem(base - steps + 8, 4), jnp.stack([second, core, core, core])[None]],
        axis=0,
    )

    def act_of(part, block):
        return lax.dynamic_slice(activations, (part * half, block * feats), (half, feats))

    own_act = [act_of(core, x), None, None, None]
    other_act = [act_of(1 - core, x), None, None, None]
    for k in (2, 1, 3):
        own_act[k] = shift_x(act_of(core, lax.rem(x + k, 4)), k)
    dictionary = load(dictionary)
    for k in (1, 3, 2):
        other_act[k] = other_core(own_act[k])

    def encode(source, before):
        def part(k):
            own, other = source(k)
            size = 512 if k == 0 else 1024
            return encode_block(own, other, index, k, dictionary, size)

        far_low, far_high = part(2)
        far_low = shift_x(far_low, 1)
        far_high = shift_x(far_high, -1)
        up_low, up_high = part(1)
        up_high = shift_x(up_high, 1)
        down_low, down_high = part(3)
        down_low = shift_x(down_low, -1)
        up_low = shift_x(add(up_low, far_low), 1)
        down_high = shift_x(add(down_high, far_high), -1)
        drives = part(0)
        received = (up_low, down_low, up_high, down_high)
        return finish(index, drives, received, before)

    def gather(coded):
        low, high = coded
        up_low = shift_x(low, 1)
        down_high = shift_x(high, -1)
        up_high = shift_x(high, 1)
        down_low = shift_x(low, -1)
        far_low = shift_x(up_low, 1)
        far_high = shift_x(down_high, -1)
        return (low, high), (up_low, up_high), (far_low, far_high), (down_low, down_high)

    def residual_of(coded):
        keeps, sent = [None] * 4, []
        for blocks in ((0,), (1, 3), (2,)):
            pieces = [piece for j in blocks for piece in coded[j]]
            kept, send = decode_blocks(pieces, dictionary, half, 1024 if blocks == (2,) else 512)
            for j, keep in zip(blocks, kept):
                keeps[j] = keep
            sent.append(other_core(send))
        routed = route(index, keeps, sent)
        pieces = [routed[0]]
        for k in (2, 1, 3):
            pieces.append(shift_mixed(routed[k], k, True))
        total = partial_sum(pieces)
        pieces = [total]
        for k in (2, 1, 3):
            pieces.append(shift_mixed(total, k, False))
        rounded, mine = residual_block(index, pieces, own_act)
        own = [rounded, None, None, None]
        other = [None] * 4
        for k in (2, 1, 3):
            own[k] = shift_mixed(rounded, k, True)
        for k in (0, 1, 3, 2):
            other[k] = other_core(own[k])
        return mine, own, other

    codes = None
    source = lambda k: (own_act[(4 - k) % 4 :][:1], other_act[(4 - k) % 4 :][:1])
    for _ in range(ITERS):
        codes, coded = encode(source, codes)
        coded = gather(coded)
        mine, own, other = residual_of(coded)
        source = lambda k, own=own, other=other: (own, other)

    residual = to_owner(mine)
    arranged = arrange(index, coded)
    turned = []
    for k in range(4):
        turned.append(turn(own[k], other[k]))
    moved, square = gradient(turned, arranged, dictionary)
    squares = [square]
    for k in (2, 1, 3):
        squares.append(shift_x(square, k))
    new_dictionary = scale(moved, squares)
    return (codes, residual, new_dictionary)


def solution(mesh):
    mesh = Mesh(mesh.devices.reshape(4, 4, 2, 4), ("z", "y", "core", "x"))
    return jax.shard_map(
        step,
        mesh=mesh,
        in_specs=(P("x", None), P("x", ATOM)),
        out_specs=(P("x", ATOM), P(ATOM, "x"), P("x", ATOM)),
        check_vma=False,
    )
```

```python
import functools

import jax
import jax.numpy as jnp
from jax import lax
from jax.experimental import pallas as pl
from jax.experimental.pallas import tpu as pltpu
from jax.sharding import Mesh, PartitionSpec as P


D = 8192
ITERS = 2
threshold = 0.05
step_size = 2.0
learn_rate = 1.0 / 16384.0
epsilon = 1e-12

BF = jnp.bfloat16
F32 = jnp.float32
ATOM = ("z", "y", "core")
MIB = 1 << 20


def shrink(values):
    return values - jnp.clip(values, -threshold, threshold)


def shift_x(value, step):
    return lax.ppermute(value, "x", [(i, (i + step) % 4) for i in range(4)])


def other_core(value):
    return lax.ppermute(value, "core", [(0, 1), (1, 0)])


def pairs_of(target):
    return [
        (z * 8 + y * 2 + core, target(z, y, core))
        for z in range(4)
        for y in range(4)
        for core in range(2)
    ]


def shift_mixed(value, step, first):
    def target(z, y, core):
        if (core == 0) == first:
            y = (y + step) % 4
        else:
            z = (z + step) % 4
        return z * 8 + y * 2 + core

    return lax.ppermute(value, ATOM, pairs_of(target))


def to_owner(value):
    def target(z, y, core):
        row, part = (y, z) if core == 0 else (z, y)
        return row * 8 + (2 * core + part // 2) * 2 + part % 2

    return lax.ppermute(value, ATOM, pairs_of(target))


def whole():
    return pl.BlockSpec(memory_space=pltpu.VMEM)


def anywhere():
    return pl.BlockSpec(memory_space=pl.ANY)


def scalars():
    return pl.BlockSpec(memory_space=pltpu.SMEM)


def in_vmem(value):
    return pltpu.with_memory_space_constraint(value, pltpu.VMEM)


def params(mib):
    return pltpu.CompilerParams(vmem_limit_bytes=mib * MIB)


def cost(flops, moved):
    return pl.CostEstimate(flops=flops, bytes_accessed=moved, transcendentals=0)


def shaped(rows, columns, dtype):
    return jax.ShapeDtypeStruct((rows, columns), dtype)


STRIP = 16


def strip(i):
    return pl.ds(pl.multiple_of(i * STRIP, STRIP), STRIP)


def fetch(index, pieces, target, sem, wait):
    for t, piece in enumerate(pieces):

        @pl.when(index == t)
        def _():
            copy = pltpu.make_async_copy(piece, target, sem)
            if wait:
                copy.wait()
            else:
                copy.start()


def load_kernel(index_ref, dict_ref, out_ref, sem):
    copy = pltpu.make_async_copy(dict_ref, out_ref, sem)
    copy.start()
    copy.wait()


def load(index, dictionary):
    return pl.pallas_call(
        load_kernel,
        in_specs=[scalars(), pl.BlockSpec(memory_space=pltpu.HBM)],
        out_specs=whole(),
        out_shape=pltpu.VMEM(dictionary.shape, BF),
        scratch_shapes=[pltpu.SemaphoreType.DMA],
        compiler_params=params(10),
        cost_estimate=cost(0, dictionary.size * 2),
        name="load",
    )(index, pltpu.with_memory_space_constraint(dictionary, pltpu.HBM))


def encode_kernel(size, ks, counted, kinds, index_ref, *refs):
    count = 4 if counted else len(ks)
    own, other = refs[:count], refs[count : 2 * count]
    dict_ref, outs = refs[2 * count], refs[2 * count + 1 : 2 * count + 1 + len(kinds)]
    left, sems = refs[-2:]
    half = own[0].shape[0]
    for wait in (False, True):
        for b, k in enumerate(ks):
            low, high = pl.ds(2 * b * half, half), pl.ds((2 * b + 1) * half, half)
            if counted:
                fetch(index_ref[k, 0], own, left.at[low], sems.at[b, 0], wait)
                fetch(index_ref[k, 1], other, left.at[high], sems.at[b, 1], wait)
            elif wait:
                left[low, :] = own[b][...]
                left[high, :] = other[b][...]

    @pl.loop(0, dict_ref.shape[1] // size)
    def _(n):
        part = pl.ds(pl.multiple_of(n * size, size), size)
        out = jnp.dot(left[...], dict_ref[:, part], preferred_element_type=F32)
        for b, ref in enumerate(outs):
            ref[:, part] = out[b * half : (b + 1) * half].astype(ref.dtype)


def encode_block(own, other, index, ks, dictionary, size):
    half, feats = own[0].shape
    atoms = dictionary.shape[1]
    kinds = []
    for k in ks:
        kinds += [BF if k in (2, 3) else F32, BF if k in (1, 2) else F32]
    counted = index is not None
    rows = 2 * half * len(ks)
    if not counted:
        index = jnp.zeros((1, 1), jnp.int32)
    return pl.pallas_call(
        functools.partial(encode_kernel, size, ks, counted, kinds),
        in_specs=[scalars()]
        + [anywhere() if counted else whole()] * (2 * len(own))
        + [whole()],
        out_specs=[whole()] * len(kinds),
        out_shape=[shaped(half, atoms, kind) for kind in kinds],
        scratch_shapes=[
            pltpu.VMEM((rows, feats), BF),
            pltpu.SemaphoreType.DMA((len(ks), 2)),
        ],
        compiler_params=params(16),
        cost_estimate=cost(2 * rows * feats * atoms, 2 * feats * atoms),
        name="encode",
    )(index, *own, *other, in_vmem(dictionary))


def add_kernel(sum_ref, piece_ref, out_ref):
    @pl.loop(0, sum_ref.shape[0] // STRIP)
    def _(i):
        here = strip(i)
        out_ref[here, :] = (sum_ref[here, :] + piece_ref[here, :].astype(F32)).astype(BF)


def add(total, piece):
    half, atoms = total.shape
    return pl.pallas_call(
        add_kernel,
        in_specs=[whole()] * 2,
        out_specs=whole(),
        out_shape=shaped(half, atoms, BF),
        compiler_params=params(8),
        cost_estimate=cost(half * atoms, 8 * half * atoms),
        name="add",
    )(in_vmem(total), piece)


def finish_kernel(last, index_ref, *refs):
    drives, received, refs = refs[:2], (refs[2:4], refs[4:6]), refs[6:]
    before_ref = refs[0] if last else None
    codes_ref, *coded = refs[-3:]
    half = drives[0].shape[0]
    strips = half // STRIP
    for h in range(2):

        @pl.loop(0, strips)
        def _(i):
            here, kept = strip(i), strip(i + h * strips)
            drive = drives[h][here, :]
            for piece in received[h]:
                drive = drive + piece[here, :].astype(F32)
            drive = step_size * drive
            codes = shrink(before_ref[kept, :] + drive if last else drive)
            there = kept
            if last:
                there = strip(lax.rem(i + (h + index_ref[4, 1]) * strips, 2 * strips))
            codes_ref[there, :] = codes
            coded[h][here, :] = codes.astype(BF)


def finish(index, drives, received, before):
    half, atoms = drives[0].shape
    last = before is not None
    codes, *coded = pl.pallas_call(
        functools.partial(finish_kernel, last),
        in_specs=[scalars()] + [whole()] * (7 if last else 6),
        out_specs=[whole()] * 3,
        out_shape=[pltpu.VMEM((2 * half, atoms), F32)] + [shaped(half, atoms, BF)] * 2,
        compiler_params=params(12),
        cost_estimate=cost(16 * half * atoms, 32 * half * atoms),
        name="finish",
    )(index, *drives, *received, *([in_vmem(before)] if last else []))
    return codes, coded


def decode_kernel(size, count, *refs):
    coded, dict_ref, keeps = refs[: 2 * count], refs[2 * count], refs[2 * count + 1 : -2]
    send_ref, left = refs[-2:]
    half = coded[0].shape[0]
    for b, piece in enumerate(coded):
        left[pl.ds(b * half, half), :] = piece[...]

    @pl.loop(0, dict_ref.shape[0] // size)
    def _(n):
        part = pl.ds(pl.multiple_of(n * size, size), size)
        recon = lax.dot_general(
            left[...], dict_ref[part, :], (((1,), (1,)), ((), ())), preferred_element_type=F32
        )
        for b, keep in enumerate(keeps):
            keep[:, part] = recon[b * half : (b + 1) * half]
        send_ref[:, part] = recon[count * half :].astype(BF)


def decode_blocks(low, high, dictionary, size):
    feats, atoms = dictionary.shape
    half, count = low[0].shape[0], len(low)
    rows = 2 * count * half
    outs = pl.pallas_call(
        functools.partial(decode_kernel, size, count),
        in_specs=[whole()] * (2 * count + 1),
        out_specs=[whole()] * (count + 1),
        out_shape=[shaped(half, feats, F32)] * count + [shaped(rows // 2, feats, BF)],
        scratch_shapes=[pltpu.VMEM((rows, atoms), BF)],
        compiler_params=params(16),
        cost_estimate=cost(2 * rows * feats * atoms, 2 * feats * atoms),
        name="decode",
    )(*low, *high, in_vmem(dictionary))
    return outs[:-1], outs[-1]


def route_kernel(index_ref, *refs):
    keeps, (sent_own, sent_down, sent_rest), outs = refs[:4], refs[4:7], refs[7:]
    half = outs[0].shape[0]
    sources = [(sent_own, 0), (sent_rest, 0), (sent_rest, half), (sent_down, 0)]
    for j in range(4):
        source, base = sources[j]
        for k in range(4):

            @pl.when(index_ref[k, 2] == j)
            def _():
                @pl.loop(0, half // STRIP)
                def _(i):
                    there = pl.ds(pl.multiple_of(base + i * STRIP, STRIP), STRIP)
                    value = keeps[j][strip(i), :] + source[there, :].astype(F32)
                    outs[k][strip(i), :] = value.astype(BF)


def route(index, keeps, sent):
    half, feats = keeps[0].shape
    return pl.pallas_call(
        route_kernel,
        in_specs=[scalars()] + [whole()] * 7,
        out_specs=[whole()] * 4,
        out_shape=[shaped(half, feats, BF)] * 4,
        compiler_params=params(12),
        cost_estimate=cost(8 * half * feats, 32 * half * feats),
        name="route",
    )(index, *(in_vmem(keep) for keep in keeps), *sent)


def total_of(pieces, here):
    total = pieces[0][here, :].astype(F32)
    for piece in pieces[1:]:
        total = total + piece[here, :].astype(F32)
    return total


def partial_kernel(*refs):
    @pl.loop(0, refs[0].shape[0] // STRIP)
    def _(i):
        refs[-1][strip(i), :] = total_of(refs[:-1], strip(i)).astype(BF)


def partial_sum(pieces):
    half, feats = pieces[0].shape
    return pl.pallas_call(
        partial_kernel,
        in_specs=[whole()] * 4,
        out_specs=whole(),
        out_shape=shaped(half, feats, BF),
        compiler_params=params(8),
        cost_estimate=cost(4 * half * feats, 10 * half * feats),
        name="partial",
    )(*pieces)


def residual_kernel(index_ref, *refs):
    pieces, acts = refs[:4], refs[4:8]
    rounded_ref, mine_ref, act, sem = refs[8:]
    for wait in (False, True):
        fetch(index_ref[0, 2], acts, act, sem, wait)

    @pl.loop(0, act.shape[0] // STRIP)
    def _(i):
        here = strip(i)
        full = act[here, :].astype(F32) - total_of(pieces, here)
        rounded_ref[here, :] = full.astype(BF)

        @pl.when(i == index_ref[4, 0])
        def _():
            mine_ref[...] = full


def residual_block(index, pieces, acts):
    half, feats = pieces[0].shape
    return pl.pallas_call(
        residual_kernel,
        in_specs=[scalars()] + [whole()] * 4 + [anywhere()] * 4,
        out_specs=[whole()] * 2,
        out_shape=[shaped(half, feats, BF), shaped(STRIP, feats, F32)],
        scratch_shapes=[pltpu.VMEM((half, feats), BF), pltpu.SemaphoreType.DMA],
        compiler_params=params(8),
        cost_estimate=cost(5 * half * feats, 14 * half * feats),
        name="residual",
    )(index, *pieces, *acts)


def arrange_kernel(index_ref, *refs):
    low, high, out_ref, sems = refs[:4], refs[4:8], refs[8], refs[9]
    half = low[0].shape[0]
    for wait in (False, True):
        for k in range(4):
            back = (4 - k) % 4
            own, other = pl.ds(2 * k * half, half), pl.ds((2 * k + 1) * half, half)
            fetch(index_ref[back, 2], low, out_ref.at[own], sems.at[k, 0], wait)
            fetch(index_ref[back, 3], high, out_ref.at[other], sems.at[k, 1], wait)


def arrange(index, coded):
    half, atoms = coded[0][0].shape
    low, high = zip(*coded)
    return pl.pallas_call(
        arrange_kernel,
        in_specs=[scalars()] + [anywhere()] * 8,
        out_specs=whole(),
        out_shape=pltpu.VMEM((8 * half, atoms), BF),
        scratch_shapes=[pltpu.SemaphoreType.DMA((4, 2))],
        compiler_params=params(8),
        cost_estimate=cost(0, 32 * half * atoms),
        name="arrange",
    )(index, *low, *high)


def turn_kernel(own_ref, other_ref, out_ref):
    out_ref[...] = jnp.concatenate([own_ref[...], other_ref[...]], axis=0).T


def turn(own, other):
    half, feats = own.shape
    return pl.pallas_call(
        turn_kernel,
        in_specs=[whole()] * 2,
        out_specs=whole(),
        out_shape=pltpu.VMEM((feats, 2 * half), BF),
        compiler_params=params(8),
        cost_estimate=cost(0, 8 * half * feats),
        name="turn",
    )(own, other)


def gradient_kernel(*refs):
    turned, (codes_ref, dict_ref, moved_ref, square_ref) = refs[:4], refs[4:]
    feats = dict_ref.shape[0]
    size, block = 512, 512

    @pl.loop(0, dict_ref.shape[1] // size)
    def _(n):
        part = pl.ds(pl.multiple_of(n * size, size), size)
        codes = codes_ref[:, part]
        total = jnp.zeros((8, size), F32)
        for f in range(feats // block):
            rows = pl.ds(f * block, block)
            left = jnp.concatenate([piece[rows, :] for piece in turned], axis=1)
            grad = jnp.dot(left, codes, preferred_element_type=F32)
            moved = dict_ref[rows, part].astype(F32) + learn_rate * grad
            moved_ref[rows, part] = moved
            total = total + jnp.sum((moved * moved).reshape(block // 8, 8, size), axis=0)
        square_ref[:, part] = jnp.sum(total, axis=0, keepdims=True)


def gradient(turned, codes, dictionary):
    feats, atoms = dictionary.shape
    rows = codes.shape[0]
    return pl.pallas_call(
        gradient_kernel,
        in_specs=[whole()] * 6,
        out_specs=[whole()] * 2,
        out_shape=[pltpu.VMEM((feats, atoms), F32), pltpu.VMEM((1, atoms), F32)],
        compiler_params=params(30),
        cost_estimate=cost(2 * rows * feats * atoms, 6 * feats * atoms),
        name="gradient",
    )(*(in_vmem(piece) for piece in turned), in_vmem(codes), in_vmem(dictionary))


def scale_kernel(moved_ref, *refs):
    squares, (out_ref, ready, sems) = refs[:4], refs[4:]
    square = squares[0][...] + squares[1][...] + squares[2][...] + squares[3][...]
    factor = lax.rsqrt(square / D + epsilon)
    count, block, _ = ready.shape
    copies = []
    for n in range(count):
        rows = pl.ds(n * block, block)

        @pl.loop(0, block // STRIP)
        def _(i):
            from_rows = pl.ds(pl.multiple_of(n * block + i * STRIP, STRIP), STRIP)
            ready[n, strip(i), :] = (moved_ref[from_rows, :] * factor).astype(BF)

        copies.append(pltpu.make_async_copy(ready.at[n], out_ref.at[rows], sems.at[n]))
        copies[n].start()
    for copy in copies:
        copy.wait()


def scale(moved, squares):
    feats, atoms = moved.shape
    count = 8
    return pl.pallas_call(
        scale_kernel,
        in_specs=[whole()] * 5,
        out_specs=pl.BlockSpec(memory_space=pltpu.HBM),
        out_shape=shaped(feats, atoms, BF),
        scratch_shapes=[
            pltpu.VMEM((count, feats // count, atoms), BF),
            pltpu.SemaphoreType.DMA((count,)),
        ],
        compiler_params=params(16),
        cost_estimate=cost(feats * atoms, feats * atoms * 2),
        name="scale",
    )(in_vmem(moved), *(in_vmem(square) for square in squares))


def store_kernel(value_ref, out_ref, sem):
    copy = pltpu.make_async_copy(value_ref, out_ref, sem)
    copy.start()
    copy.wait()


def store(value):
    return pl.pallas_call(
        store_kernel,
        in_specs=[whole()],
        out_specs=pl.BlockSpec(memory_space=pltpu.HBM),
        out_shape=jax.ShapeDtypeStruct(value.shape, value.dtype),
        scratch_shapes=[pltpu.SemaphoreType.DMA],
        compiler_params=params(4),
        cost_estimate=cost(0, 4 * value.size),
        name="store",
    )(in_vmem(value))


def step(activations, dictionary):
    x = lax.axis_index("x")
    y = lax.axis_index("y")
    z = lax.axis_index("z")
    core = lax.axis_index("core")
    first = jnp.where(core == 0, y, z)
    second = jnp.where(core == 0, z, y)
    rows = activations.shape[0]
    feats = dictionary.shape[0]
    half = rows // 2
    steps = jnp.arange(4, dtype=jnp.int32)[:, None]
    base = jnp.stack([first - x, second - x, x - first, x - second])[None]
    index = jnp.concatenate(
        [lax.rem(base - steps + 8, 4), jnp.stack([second, core, core, core])[None]],
        axis=0,
    )

    def act_of(part, block):
        return lax.dynamic_slice(activations, (part * half, block * feats), (half, feats))

    own_act = [act_of(core, x), None, None, None]
    other_act = [act_of(1 - core, x), None, None, None]
    for k in (2, 1, 3):
        own_act[k] = shift_x(act_of(core, lax.rem(x + k, 4)), k)
    dictionary = load(index, dictionary)
    for k in (1, 3, 2):
        other_act[k] = other_core(own_act[k])

    def encode(source, before):
        def part(*ks):
            own, other = source(ks)
            size = 512 if ks == (0,) else 1024
            return encode_block(own, other, None if before is None else index, ks, dictionary, size)

        far_low, far_high = part(2)
        far_low = shift_x(far_low, 1)
        far_high = shift_x(far_high, -1)
        up_low, up_high, down_low, down_high = part(1, 3)
        up_high = shift_x(up_high, 1)
        down_low = shift_x(down_low, -1)
        up_low = shift_x(add(up_low, far_low), 1)
        down_high = shift_x(add(down_high, far_high), -1)
        drives = part(0)
        received = (up_low, down_low, up_high, down_high)
        return finish(index, drives, received, before)

    def gather(coded):
        low, high = coded
        up_low = shift_x(low, 1)
        down_high = shift_x(high, -1)
        up_high = shift_x(high, 1)
        down_low = shift_x(low, -1)
        far_low = shift_x(up_low, 1)
        far_high = shift_x(down_high, -1)
        return (low, high), (up_low, up_high), (far_low, far_high), (down_low, down_high)

    def residual_of(coded):
        keeps, sent = [None] * 4, []
        groups = (((0,), (0,)), ((1,), (3,)), ((3, 2), (1, 2)))
        for g, (low, high) in enumerate(groups):
            kept, send = decode_blocks(
                [coded[j][0] for j in low],
                [coded[j][1] for j in high],
                dictionary,
                1024 if g == 2 else 512,
            )
            for j, keep in zip(low, kept):
                keeps[j] = keep
            sent.append(other_core(send))
        routed = route(index, keeps, sent)
        pieces = [routed[0]]
        for k in (2, 1, 3):
            pieces.append(shift_mixed(routed[k], k, True))
        total = partial_sum(pieces)
        pieces = [total]
        for k in (2, 1, 3):
            pieces.append(shift_mixed(total, k, False))
        rounded, mine = residual_block(index, pieces, own_act)
        own = [rounded, None, None, None]
        other = [None] * 4
        for k in (2, 1, 3):
            own[k] = shift_mixed(rounded, k, True)
        for k in (0, 1, 3, 2):
            other[k] = other_core(own[k])
        return mine, own, other

    codes = None
    source = lambda ks: (
        [own_act[(4 - k) % 4] for k in ks],
        [other_act[(4 - k) % 4] for k in ks],
    )
    for _ in range(ITERS):
        codes, coded = encode(source, codes)
        coded = gather(coded)
        mine, own, other = residual_of(coded)
        source = lambda ks, own=own, other=other: (own, other)

    residual = to_owner(mine)
    arranged = arrange(index, coded)
    turned = []
    for k in range(4):
        turned.append(turn(own[k], other[k]))
    moved, square = gradient(turned, arranged, dictionary)
    squares = [square]
    for k in (2, 1, 3):
        squares.append(shift_x(square, k))
    new_dictionary = scale(moved, squares)
    codes = store(codes)
    residual = store(residual)
    return (codes, residual, new_dictionary)


def solution(mesh):
    mesh = Mesh(mesh.devices.reshape(4, 4, 2, 4), ("z", "y", "core", "x"))
    return jax.shard_map(
        step,
        mesh=mesh,
        in_specs=(P("x", None), P("x", ATOM)),
        out_specs=(P("x", ATOM), P(ATOM, "x"), P("x", ATOM)),
        check_vma=False,
    )
```

```python
import functools

import jax
import jax.numpy as jnp
from jax import lax
from jax.experimental import pallas as pl
from jax.experimental.pallas import tpu as pltpu
from jax.sharding import Mesh, PartitionSpec as P


D = 8192
ITERS = 2
threshold = 0.05
step_size = 2.0
learn_rate = 1.0 / 16384.0
epsilon = 1e-12

BF = jnp.bfloat16
F32 = jnp.float32
ATOM = ("z", "y", "core")
MIB = 1 << 20


def shrink(values):
    return values - jnp.clip(values, -threshold, threshold)


def shift_x(value, step):
    return lax.ppermute(value, "x", [(i, (i + step) % 4) for i in range(4)])


def other_core(value):
    return lax.ppermute(value, "core", [(0, 1), (1, 0)])


def pairs_of(target):
    return [
        (z * 8 + y * 2 + core, target(z, y, core))
        for z in range(4)
        for y in range(4)
        for core in range(2)
    ]


def shift_mixed(value, step, first):
    def target(z, y, core):
        if (core == 0) == first:
            y = (y + step) % 4
        else:
            z = (z + step) % 4
        return z * 8 + y * 2 + core

    return lax.ppermute(value, ATOM, pairs_of(target))


def to_owner(value):
    def target(z, y, core):
        row, part = (y, z) if core == 0 else (z, y)
        return row * 8 + (2 * core + part // 2) * 2 + part % 2

    return lax.ppermute(value, ATOM, pairs_of(target))


def whole():
    return pl.BlockSpec(memory_space=pltpu.VMEM)


def anywhere():
    return pl.BlockSpec(memory_space=pl.ANY)


def scalars():
    return pl.BlockSpec(memory_space=pltpu.SMEM)


def in_vmem(value):
    return pltpu.with_memory_space_constraint(value, pltpu.VMEM)


def params(mib):
    return pltpu.CompilerParams(vmem_limit_bytes=mib * MIB)


def cost(flops, moved):
    return pl.CostEstimate(flops=flops, bytes_accessed=moved, transcendentals=0)


def shaped(rows, columns, dtype):
    return jax.ShapeDtypeStruct((rows, columns), dtype)


STRIP = 16


def strip(i):
    return pl.ds(pl.multiple_of(i * STRIP, STRIP), STRIP)


def fetch(index, pieces, target, sem, wait):
    for t, piece in enumerate(pieces):

        @pl.when(index == t)
        def _():
            copy = pltpu.make_async_copy(piece, target, sem)
            if wait:
                copy.wait()
            else:
                copy.start()


def load_kernel(index_ref, dict_ref, out_ref, sem):
    copy = pltpu.make_async_copy(dict_ref, out_ref, sem)
    copy.start()
    copy.wait()


def load(index, dictionary):
    return pl.pallas_call(
        load_kernel,
        in_specs=[scalars(), pl.BlockSpec(memory_space=pltpu.HBM)],
        out_specs=whole(),
        out_shape=pltpu.VMEM(dictionary.shape, BF),
        scratch_shapes=[pltpu.SemaphoreType.DMA],
        compiler_params=params(10),
        cost_estimate=cost(0, dictionary.size * 2),
        name="load",
    )(index, pltpu.with_memory_space_constraint(dictionary, pltpu.HBM))


def encode_kernel(size, ks, counted, kinds, index_ref, *refs):
    count = 4 if counted else len(ks)
    own, other = refs[:count], refs[count : 2 * count]
    dict_ref, outs = refs[2 * count], refs[2 * count + 1 : 2 * count + 1 + len(kinds)]
    left, sems = refs[-2:]
    half = own[0].shape[0]
    for wait in (False, True):
        for b, k in enumerate(ks):
            low, high = pl.ds(2 * b * half, half), pl.ds((2 * b + 1) * half, half)
            if counted:
                fetch(index_ref[k, 0], own, left.at[low], sems.at[b, 0], wait)
                fetch(index_ref[k, 1], other, left.at[high], sems.at[b, 1], wait)
            elif wait:
                left[low, :] = own[b][...]
                left[high, :] = other[b][...]

    @pl.loop(0, dict_ref.shape[1] // size)
    def _(n):
        part = pl.ds(pl.multiple_of(n * size, size), size)
        out = jnp.dot(left[...], dict_ref[:, part], preferred_element_type=F32)
        for b, ref in enumerate(outs):
            ref[:, part] = out[b * half : (b + 1) * half].astype(ref.dtype)


def encode_block(own, other, index, ks, dictionary, size):
    half, feats = own[0].shape
    atoms = dictionary.shape[1]
    kinds = []
    for k in ks:
        kinds += [BF if k in (2, 3) else F32, BF if k in (1, 2) else F32]
    counted = index is not None
    rows = 2 * half * len(ks)
    if not counted:
        index = jnp.zeros((1, 1), jnp.int32)
    return pl.pallas_call(
        functools.partial(encode_kernel, size, ks, counted, kinds),
        in_specs=[scalars()]
        + [anywhere() if counted else whole()] * (2 * len(own))
        + [whole()],
        out_specs=[whole()] * len(kinds),
        out_shape=[shaped(half, atoms, kind) for kind in kinds],
        scratch_shapes=[
            pltpu.VMEM((rows, feats), BF),
            pltpu.SemaphoreType.DMA((len(ks), 2)),
        ],
        compiler_params=params(16),
        cost_estimate=cost(2 * rows * feats * atoms, 2 * feats * atoms),
        name="encode",
    )(index, *own, *other, in_vmem(dictionary))


def add_kernel(sum_ref, piece_ref, out_ref):
    @pl.loop(0, sum_ref.shape[0] // STRIP)
    def _(i):
        here = strip(i)
        out_ref[here, :] = (sum_ref[here, :] + piece_ref[here, :].astype(F32)).astype(BF)


def add(total, piece):
    half, atoms = total.shape
    return pl.pallas_call(
        add_kernel,
        in_specs=[whole()] * 2,
        out_specs=whole(),
        out_shape=shaped(half, atoms, BF),
        compiler_params=params(8),
        cost_estimate=cost(half * atoms, 8 * half * atoms),
        name="add",
    )(in_vmem(total), piece)


def finish_kernel(last, index_ref, *refs):
    drives, received, refs = refs[:2], (refs[2:4], refs[4:6]), refs[6:]
    before_ref = refs[0] if last else None
    codes_ref, *coded = refs[-3:]
    half = drives[0].shape[0]
    strips = half // STRIP
    for h in range(2):

        @pl.loop(0, strips)
        def _(i):
            here, kept = strip(i), strip(i + h * strips)
            drive = drives[h][here, :]
            for piece in received[h]:
                drive = drive + piece[here, :].astype(F32)
            drive = step_size * drive
            codes = shrink(before_ref[kept, :] + drive if last else drive)
            there = kept
            if last:
                there = strip(lax.rem(i + (h + index_ref[4, 1]) * strips, 2 * strips))
            codes_ref[there, :] = codes
            coded[h][here, :] = codes.astype(BF)


def finish(index, drives, received, before):
    half, atoms = drives[0].shape
    last = before is not None
    codes, *coded = pl.pallas_call(
        functools.partial(finish_kernel, last),
        in_specs=[scalars()] + [whole()] * (7 if last else 6),
        out_specs=[whole()] * 3,
        out_shape=[pltpu.VMEM((2 * half, atoms), F32)] + [shaped(half, atoms, BF)] * 2,
        compiler_params=params(12),
        cost_estimate=cost(16 * half * atoms, 32 * half * atoms),
        name="finish",
    )(index, *drives, *received, *([in_vmem(before)] if last else []))
    return codes, coded


def decode_kernel(size, count, *refs):
    coded, dict_ref, keeps = refs[: 2 * count], refs[2 * count], refs[2 * count + 1 : -2]
    send_ref, left = refs[-2:]
    half = coded[0].shape[0]
    for b, piece in enumerate(coded):
        left[pl.ds(b * half, half), :] = piece[...]

    @pl.loop(0, dict_ref.shape[0] // size)
    def _(n):
        part = pl.ds(pl.multiple_of(n * size, size), size)
        recon = lax.dot_general(
            left[...], dict_ref[part, :], (((1,), (1,)), ((), ())), preferred_element_type=F32
        )
        for b, keep in enumerate(keeps):
            keep[:, part] = recon[b * half : (b + 1) * half]
        send_ref[:, part] = recon[count * half :].astype(BF)


def decode_blocks(low, high, dictionary, size):
    feats, atoms = dictionary.shape
    half, count = low[0].shape[0], len(low)
    rows = 2 * count * half
    outs = pl.pallas_call(
        functools.partial(decode_kernel, size, count),
        in_specs=[whole()] * (2 * count + 1),
        out_specs=[whole()] * (count + 1),
        out_shape=[shaped(half, feats, F32)] * count + [shaped(rows // 2, feats, BF)],
        scratch_shapes=[pltpu.VMEM((rows, atoms), BF)],
        compiler_params=params(16),
        cost_estimate=cost(2 * rows * feats * atoms, 2 * feats * atoms),
        name="decode",
    )(*low, *high, in_vmem(dictionary))
    return outs[:-1], outs[-1]


def route_kernel(index_ref, *refs):
    keeps, (sent_own, sent_down, sent_rest), outs = refs[:4], refs[4:7], refs[7:]
    half = outs[0].shape[0]
    sources = [(sent_own, 0), (sent_rest, 0), (sent_rest, half), (sent_down, 0)]
    for j in range(4):
        source, base = sources[j]
        for k in range(4):

            @pl.when(index_ref[k, 2] == j)
            def _():
                @pl.loop(0, half // STRIP)
                def _(i):
                    there = pl.ds(pl.multiple_of(base + i * STRIP, STRIP), STRIP)
                    value = keeps[j][strip(i), :] + source[there, :].astype(F32)
                    outs[k][strip(i), :] = value.astype(BF)


def route(index, keeps, sent):
    half, feats = keeps[0].shape
    return pl.pallas_call(
        route_kernel,
        in_specs=[scalars()] + [whole()] * 7,
        out_specs=[whole()] * 4,
        out_shape=[shaped(half, feats, BF)] * 4,
        compiler_params=params(12),
        cost_estimate=cost(8 * half * feats, 32 * half * feats),
        name="route",
    )(index, *(in_vmem(keep) for keep in keeps), *sent)


def total_of(pieces, here):
    total = pieces[0][here, :].astype(F32)
    for piece in pieces[1:]:
        total = total + piece[here, :].astype(F32)
    return total


def partial_kernel(*refs):
    @pl.loop(0, refs[0].shape[0] // STRIP)
    def _(i):
        refs[-1][strip(i), :] = total_of(refs[:-1], strip(i)).astype(BF)


def partial_sum(pieces):
    half, feats = pieces[0].shape
    return pl.pallas_call(
        partial_kernel,
        in_specs=[whole()] * 4,
        out_specs=whole(),
        out_shape=shaped(half, feats, BF),
        compiler_params=params(8),
        cost_estimate=cost(4 * half * feats, 10 * half * feats),
        name="partial",
    )(*pieces)


def residual_kernel(index_ref, *refs):
    pieces, acts = refs[:4], refs[4:8]
    rounded_ref, mine_ref, act, sem = refs[8:]
    for wait in (False, True):
        fetch(index_ref[0, 2], acts, act, sem, wait)

    @pl.loop(0, act.shape[0] // STRIP)
    def _(i):
        here = strip(i)
        full = act[here, :].astype(F32) - total_of(pieces, here)
        rounded_ref[here, :] = full.astype(BF)

        @pl.when(i == index_ref[4, 0])
        def _():
            mine_ref[...] = full


def residual_block(index, pieces, acts):
    half, feats = pieces[0].shape
    return pl.pallas_call(
        residual_kernel,
        in_specs=[scalars()] + [whole()] * 4 + [anywhere()] * 4,
        out_specs=[whole()] * 2,
        out_shape=[shaped(half, feats, BF), shaped(STRIP, feats, F32)],
        scratch_shapes=[pltpu.VMEM((half, feats), BF), pltpu.SemaphoreType.DMA],
        compiler_params=params(8),
        cost_estimate=cost(5 * half * feats, 14 * half * feats),
        name="residual",
    )(index, *pieces, *acts)


def arrange_kernel(index_ref, *refs):
    low, high, out_ref, sems = refs[:4], refs[4:8], refs[8], refs[9]
    half = low[0].shape[0]
    for wait in (False, True):
        for k in range(4):
            back = (4 - k) % 4
            own, other = pl.ds(2 * k * half, half), pl.ds((2 * k + 1) * half, half)
            fetch(index_ref[back, 2], low, out_ref.at[own], sems.at[k, 0], wait)
            fetch(index_ref[back, 3], high, out_ref.at[other], sems.at[k, 1], wait)


def arrange(index, coded):
    half, atoms = coded[0][0].shape
    low, high = zip(*coded)
    return pl.pallas_call(
        arrange_kernel,
        in_specs=[scalars()] + [anywhere()] * 8,
        out_specs=whole(),
        out_shape=pltpu.VMEM((8 * half, atoms), BF),
        scratch_shapes=[pltpu.SemaphoreType.DMA((4, 2))],
        compiler_params=params(8),
        cost_estimate=cost(0, 32 * half * atoms),
        name="arrange",
    )(index, *low, *high)


def turn_kernel(own_ref, other_ref, out_ref):
    out_ref[...] = jnp.concatenate([own_ref[...], other_ref[...]], axis=0).T


def turn(own, other):
    half, feats = own.shape
    return pl.pallas_call(
        turn_kernel,
        in_specs=[whole()] * 2,
        out_specs=whole(),
        out_shape=pltpu.VMEM((feats, 2 * half), BF),
        compiler_params=params(8),
        cost_estimate=cost(0, 8 * half * feats),
        name="turn",
    )(own, other)


def gradient_kernel(*refs):
    turned, (codes_ref, dict_ref, moved_ref, square_ref) = refs[:4], refs[4:]
    feats = dict_ref.shape[0]
    size, block = 512, 512

    @pl.loop(0, dict_ref.shape[1] // size)
    def _(n):
        part = pl.ds(pl.multiple_of(n * size, size), size)
        codes = codes_ref[:, part]
        total = jnp.zeros((8, size), F32)
        for f in range(feats // block):
            rows = pl.ds(f * block, block)
            left = jnp.concatenate([piece[rows, :] for piece in turned], axis=1)
            grad = jnp.dot(left, codes, preferred_element_type=F32)
            moved = dict_ref[rows, part].astype(F32) + learn_rate * grad
            moved_ref[rows, part] = moved
            total = total + jnp.sum((moved * moved).reshape(block // 8, 8, size), axis=0)
        square_ref[:, part] = jnp.sum(total, axis=0, keepdims=True)


def gradient(turned, codes, dictionary):
    feats, atoms = dictionary.shape
    rows = codes.shape[0]
    return pl.pallas_call(
        gradient_kernel,
        in_specs=[whole()] * 6,
        out_specs=[whole()] * 2,
        out_shape=[pltpu.VMEM((feats, atoms), F32), pltpu.VMEM((1, atoms), F32)],
        compiler_params=params(30),
        cost_estimate=cost(2 * rows * feats * atoms, 6 * feats * atoms),
        name="gradient",
    )(*(in_vmem(piece) for piece in turned), in_vmem(codes), in_vmem(dictionary))


def scale_kernel(moved_ref, *refs):
    squares, (out_ref, ready, sems) = refs[:4], refs[4:]
    square = squares[0][...] + squares[1][...] + squares[2][...] + squares[3][...]
    factor = lax.rsqrt(square / D + epsilon)
    count, block, _ = ready.shape
    copies = []
    for n in range(count):
        rows = pl.ds(n * block, block)

        @pl.loop(0, block // STRIP)
        def _(i):
            from_rows = pl.ds(pl.multiple_of(n * block + i * STRIP, STRIP), STRIP)
            ready[n, strip(i), :] = (moved_ref[from_rows, :] * factor).astype(BF)

        copies.append(pltpu.make_async_copy(ready.at[n], out_ref.at[rows], sems.at[n]))
        copies[n].start()
    for copy in copies:
        copy.wait()


def scale(moved, squares):
    feats, atoms = moved.shape
    count = 8
    return pl.pallas_call(
        scale_kernel,
        in_specs=[whole()] * 5,
        out_specs=pl.BlockSpec(memory_space=pltpu.HBM),
        out_shape=shaped(feats, atoms, BF),
        scratch_shapes=[
            pltpu.VMEM((count, feats // count, atoms), BF),
            pltpu.SemaphoreType.DMA((count,)),
        ],
        compiler_params=params(16),
        cost_estimate=cost(feats * atoms, feats * atoms * 2),
        name="scale",
    )(in_vmem(moved), *(in_vmem(square) for square in squares))


def store_kernel(value_ref, out_ref, sem):
    copy = pltpu.make_async_copy(value_ref, out_ref, sem)
    copy.start()
    copy.wait()


def store(value):
    return pl.pallas_call(
        store_kernel,
        in_specs=[whole()],
        out_specs=pl.BlockSpec(memory_space=pltpu.HBM),
        out_shape=jax.ShapeDtypeStruct(value.shape, value.dtype),
        scratch_shapes=[pltpu.SemaphoreType.DMA],
        compiler_params=params(4),
        cost_estimate=cost(0, 4 * value.size),
        name="store",
    )(in_vmem(value))


def step(activations, dictionary):
    x = lax.axis_index("x")
    y = lax.axis_index("y")
    z = lax.axis_index("z")
    core = lax.axis_index("core")
    first = jnp.where(core == 0, y, z)
    second = jnp.where(core == 0, z, y)
    rows = activations.shape[0]
    feats = dictionary.shape[0]
    half = rows // 2
    steps = jnp.arange(4, dtype=jnp.int32)[:, None]
    base = jnp.stack([first - x, second - x, x - first, x - second])[None]
    index = jnp.concatenate(
        [lax.rem(base - steps + 8, 4), jnp.stack([second, core, core, core])[None]],
        axis=0,
    )

    def act_of(part, block):
        return lax.dynamic_slice(activations, (part * half, block * feats), (half, feats))

    own_act = [act_of(core, x), None, None, None]
    other_act = [act_of(1 - core, x), None, None, None]
    for k in (2, 1, 3):
        own_act[k] = shift_x(act_of(core, lax.rem(x + k, 4)), k)
    dictionary = load(index, dictionary)
    for k in (1, 3, 2):
        other_act[k] = other_core(own_act[k])

    def encode(source, before):
        def part(*ks):
            own, other = source(ks)
            size = 512 if ks == (0,) else 1024
            return encode_block(own, other, None if before is None else index, ks, dictionary, size)

        far_low, far_high = part(2)
        far_low = shift_x(far_low, 1)
        far_high = shift_x(far_high, -1)
        up_low, up_high, down_low, down_high = part(1, 3)
        up_high = shift_x(up_high, 1)
        down_low = shift_x(down_low, -1)
        up_low = shift_x(add(up_low, far_low), 1)
        down_high = shift_x(add(down_high, far_high), -1)
        drives = part(0)
        received = (up_low, down_low, up_high, down_high)
        return finish(index, drives, received, before)

    def gather(coded):
        low, high = coded
        up_low = shift_x(low, 1)
        down_high = shift_x(high, -1)
        up_high = shift_x(high, 1)
        down_low = shift_x(low, -1)
        far_low = shift_x(up_low, 1)
        far_high = shift_x(down_high, -1)
        return (low, high), (up_low, up_high), (far_low, far_high), (down_low, down_high)

    def residual_of(coded, turns):
        keeps, sent = [None] * 4, []
        groups = (((0,), (0,)), ((1,), (3,)), ((3, 2), (1, 2)))
        for g, (low, high) in enumerate(groups):
            kept, send = decode_blocks(
                [coded[j][0] for j in low],
                [coded[j][1] for j in high],
                dictionary,
                1024 if g == 2 else 512,
            )
            for j, keep in zip(low, kept):
                keeps[j] = keep
            sent.append(other_core(send))
        routed = route(index, keeps, sent)
        pieces = [routed[0]]
        for k in turns:
            pieces.append(shift_mixed(routed[k], k, True))
        total = partial_sum(pieces)
        pieces = [total]
        for k in turns:
            pieces.append(shift_mixed(total, k, False))
        rounded, mine = residual_block(index, pieces, own_act)
        own = [rounded, None, None, None]
        other = [None] * 4
        for k in turns:
            own[k] = shift_mixed(rounded, k, True)
        for k in (0, 1, 3, 2):
            other[k] = other_core(own[k])
        return mine, own, other

    codes = None
    source = lambda ks: (
        [own_act[(4 - k) % 4] for k in ks],
        [other_act[(4 - k) % 4] for k in ks],
    )
    for iteration in range(ITERS):
        codes, coded = encode(source, codes)
        coded = gather(coded)
        mine, own, other = residual_of(coded, (1, 3, 2) if iteration == 0 else (2, 1, 3))
        source = lambda ks, own=own, other=other: (own, other)

    residual = to_owner(mine)
    arranged = arrange(index, coded)
    turned = []
    for k in range(4):
        turned.append(turn(own[k], other[k]))
    moved, square = gradient(turned, arranged, dictionary)
    squares = [square]
    for k in (2, 1, 3):
        squares.append(shift_x(square, k))
    new_dictionary = scale(moved, squares)
    codes = store(codes)
    residual = store(residual)
    return (codes, residual, new_dictionary)


def solution(mesh):
    mesh = Mesh(mesh.devices.reshape(4, 4, 2, 4), ("z", "y", "core", "x"))
    return jax.shard_map(
        step,
        mesh=mesh,
        in_specs=(P("x", None), P("x", ATOM)),
        out_specs=(P("x", ATOM), P(ATOM, "x"), P("x", ATOM)),
        check_vma=False,
    )
```
